512 devices in a mesh: section: 64 (over z, y_hi, core), tensor: 8 (over x, y_lo).
Axes of the slice: x: 4, y: 8 (y_hi: 4, y_lo: 2; y = y_hi * 2 + y_lo), z: 8, core: 2. Of those that a mesh axis runs over, the one named last changes fastest.
Arguments:
- grad_in: bfloat16 [64, 256, 6144], P('section', None, 'tensor'), may hold values from -6 to 6
- loss_grad: bfloat16 [256, 6144], P(None, 'tensor'), may hold values from -6 to 6
- queries: bfloat16 [64, 2, 256, 6144], P('section', None, None, 'tensor'), may hold values from -32 to 32
- attn_keys: bfloat16 [64, 2, 256, 6144], P('section', None, None, 'tensor'), may hold values from -32 to 32
- stored_input: bfloat16 [64, 2, 256, 6144], P('section', None, 'tensor'), may hold values from -6 to 6
- block_scales: bfloat16 [64, 2, 256, 48], P('section', None, 'tensor'), may hold values from 0.25 to 4
Outputs:
- grad_next: bfloat16 [64, 256, 6144], P('section', None, 'tensor')
- query_grad: bfloat16 [64, 2, 256, 6144], P('section', None, None, 'tensor')
- key_grad: bfloat16 [64, 2, 256, 6144], P('section', None, None, 'tensor')
The draws below stay inside these ranges and needn't reach their ends.
All inputs are finite; a program needn't handle non-finite values.
Results may differ from the reference program's by a relative error of at most 0.0063.
Values may be sent and summed in bfloat16 or wider, within the bound.
A program may use at most 64 MiB of HBM per device.

```python
import math
import jax
import jax.numpy as jnp
from jax import lax

HD = 128
TOK = 256
SECTIONS = 64
D = 6144
NBLOCKS = 48


def draw_pair(key):
    base = jax.random.fold_in(key, 7)
    seed_query, seed_keys = jax.random.split(base, 2)
    shape = (SECTIONS, 2, TOK, D)
    query_all = jnp.clip(jax.random.normal(seed_query, shape, jnp.float32), -6.0, 6.0)
    keys_all = jnp.clip(jax.random.normal(seed_keys, shape, jnp.float32), -6.0, 6.0)
    return (query_all, keys_all)


def draw_queries(key, part):
    return draw_pair(key)[0].astype(jnp.bfloat16)


def draw_attn_keys(key, part):
    return draw_pair(key)[1].astype(jnp.bfloat16)


def steps_of(key, dims, cuts, low, largest):
    loudness, own = 1.0, jax.random.fold_in(key, 6)
    for dim, parts in cuts:
        draws = jnp.exp(jax.random.uniform(jax.random.fold_in(own, dim), (parts,), jnp.float32, low / len(cuts), largest / len(cuts)))
        loudness = loudness * jnp.repeat(draws, dims[dim] // parts).reshape([-1 if axis == dim else 1 for axis in range(len(dims))])
    return loudness


def normal_values(own_key, shape, deviation, reach, pieces=(), held_as=jnp.bfloat16):
    values = jax.random.normal(own_key, shape, jnp.float32) * deviation
    if len(pieces) > 0:
        values = steps_of(own_key, shape, pieces, -0.22, 0.18) * values
    return jnp.clip(values, min=-reach, max=reach).astype(held_as)


def setup_inputs(seed: int = 0) -> dict:
    key_of = jax.random.split(jax.random.key(seed), 7)
    return {
        "grad_in": normal_values(key_of[0], (SECTIONS, TOK, D), 1.0, 6.0, ((0, 64), (2, 8))),
        "loss_grad": normal_values(key_of[1], (TOK, D), 1.0, 6.0, ((1, 8),)),
        "queries": draw_queries(jax.random.fold_in(key_of[6], 71), 0),
        "attn_keys": draw_attn_keys(jax.random.fold_in(key_of[6], 71), 0),
        "stored_input": normal_values(key_of[4], (SECTIONS, 2, TOK, D), 1.0, 6.0, ((0, 64), (2, 8))),
        "block_scales": jnp.clip(jnp.exp(math.log(4.0) - 2.7725887 * jax.random.uniform(key_of[5], (SECTIONS, 2, TOK, NBLOCKS), jnp.float32) ** steps_of(key_of[5], (SECTIONS, 2, TOK, NBLOCKS), ((0, 64), (2, 8)), -0.2, 0.2)), 0.25, 4.0).astype(jnp.bfloat16),
    }


def attention_weights(query_part, key_part):
    tokens = query_part.shape[0]
    heads = query_part.shape[1] // HD
    query_heads = query_part.reshape(tokens, heads, HD).astype(jnp.float32)
    key_heads = key_part.reshape(tokens, heads, HD).astype(jnp.float32)
    scores = jnp.einsum('thd,jhd->htj', query_heads, key_heads) * (1.0 / math.sqrt(HD))
    causal = lax.broadcasted_iota(jnp.int32, (tokens, tokens), 0) >= lax.broadcasted_iota(jnp.int32, (tokens, tokens), 1)
    scores = jnp.where(causal[None], scores, -1e+30)
    scores = scores - lax.optimization_barrier(jnp.max(scores, axis=-1, keepdims=True))
    expon = jnp.exp(scores)
    return expon / lax.optimization_barrier(jnp.sum(expon, axis=-1, keepdims=True))

def value_grad(weights, upstream):
    tokens, width = upstream.shape
    rounded = weights.astype(jnp.bfloat16).astype(jnp.float32)
    upstream_heads = upstream.reshape(tokens, width // HD, HD).astype(jnp.float32)
    carried = jnp.einsum('htj,thd->jhd', rounded, upstream_heads)
    return (upstream.astype(jnp.float32) + carried.reshape(tokens, width)).astype(jnp.bfloat16)

def score_grads(weights, upstream, inputs, query_part, key_part):
    tokens, width = upstream.shape
    heads = width // HD
    upstream_heads = upstream.reshape(tokens, heads, HD).astype(jnp.float32)
    input_heads = inputs.reshape(tokens, heads, HD).astype(jnp.float32)
    product = jnp.einsum('thd,jhd->htj', upstream_heads, input_heads)
    centre = lax.optimization_barrier(jnp.sum(weights * product, axis=-1, keepdims=True))
    score_diff = (weights * (product - centre)).astype(jnp.bfloat16).astype(jnp.float32)
    scaling = 1.0 / math.sqrt(HD)
    key_heads = key_part.reshape(tokens, heads, HD).astype(jnp.float32)
    query_heads = query_part.reshape(tokens, heads, HD).astype(jnp.float32)
    query_out = (jnp.einsum('htj,jhd->thd', score_diff, key_heads) * scaling).reshape(tokens, width).astype(jnp.bfloat16)
    key_out = (jnp.einsum('htj,thd->jhd', score_diff, query_heads) * scaling).reshape(tokens, width).astype(jnp.bfloat16)
    return (query_out, key_out)

def dequantize(values, scales):
    wide = jnp.repeat(scales.astype(jnp.float32), HD, axis=-1)
    return (values.astype(jnp.float32) * wide).astype(jnp.bfloat16)

def reference(grad_in, loss_grad, queries, attn_keys, stored_input, block_scales):

    def first(items):
        upstream, query_pair, key_pair = items
        return value_grad(attention_weights(query_pair[0], key_pair[0]), upstream)
    input_first = lax.map(first, (grad_in, queries, attn_keys))
    grad_second = jnp.concatenate([input_first[1:], loss_grad[None]], axis=0)

    def second(items):
        upstream_first, upstream_second, query_pair, key_pair, values, scales = items
        weights_first = attention_weights(query_pair[0], key_pair[0])
        weights_second = attention_weights(query_pair[1], key_pair[1])
        input_second = value_grad(weights_second, upstream_second)
        inputs_first = dequantize(values[0], scales[0])
        inputs_second = dequantize(values[1], scales[1])
        query_first, key_first = score_grads(weights_first, upstream_first, inputs_first, query_pair[0], key_pair[0])
        query_second, key_second = score_grads(weights_second, upstream_second, inputs_second, query_pair[1], key_pair[1])
        return (input_second, jnp.stack([query_first, query_second]), jnp.stack([key_first, key_second]))
    input_second, query_grad, key_grad = lax.map(second, (grad_in, grad_second, queries, attn_keys, stored_input, block_scales))
    grad_next = jnp.concatenate([input_second[1:], jnp.zeros_like(input_second[:1])], axis=0)
    return (grad_next, query_grad, key_grad)
```

```python
import functools
import math

import jax
import jax.numpy as jnp
from jax import lax
from jax.experimental import pallas as pl
from jax.experimental.pallas import tpu as pltpu
from jax.sharding import PartitionSpec as P

HD = 128
SCALING = 1.0 / math.sqrt(HD)
EXP2_SCALE = SCALING * math.log2(math.e)
MESH = pl.DeviceIdType.MESH
STEPS = ((0, 1), (1, 1), (3, 1), (2, 1), (1, 0), (3, 0), (2, 0))


def across(a, b, dims):
    return lax.dot_general(a, b, (dims, ((), ())), preferred_element_type=jnp.float32)


def kernel(
    sections, heads,
    g_hbm, loss_hbm, q_hbm, k_hbm, x_hbm, s_hbm,
    next_hbm, qg_hbm, kg_hbm,
    xv, sv, gv, qv, kv, xs, xr, w, d0, d1, qo, ko,
    x_sem, s_sem, g_sem, q_sem, k_sem, own_sem, a2a_send, a2a_recv,
    r0_send, r1_send, r1_recv, qo_sem, ko_sem,
):
    section = lax.axis_index("section")
    me = lax.axis_index("tensor")
    x_me, y_me = me // 2, me % 2
    tokens = gv.shape[1]
    before = (section + sections - 1) % sections
    after = (section + 1) % sections
    is_last = section == sections - 1
    both = 2 * heads

    def partner(step, sign):
        dx, dy = step
        return ((x_me + 4 + sign * dx) % 4) * 2 + (y_me + dy) % 2

    def columns(h):
        return pl.ds(pl.multiple_of(h * HD, HD), HD)

    def q_copy(m, h):
        i = m * heads + h
        return pltpu.make_async_copy(q_hbm.at[0, m, :, columns(h)], qv.at[i], q_sem.at[i])

    def k_copy(m, h):
        i = m * heads + h
        return pltpu.make_async_copy(k_hbm.at[0, m, :, columns(h)], kv.at[i], k_sem.at[i])

    def g_copy(h):
        return pltpu.make_async_copy(g_hbm.at[0, :, columns(h)], gv.at[h], g_sem.at[h])

    def loss_copy(h):
        return pltpu.make_async_copy(
            loss_hbm.at[:, columns(h)], gv.at[heads + h], g_sem.at[heads + h]
        )

    def relay0(h):
        return pltpu.make_async_remote_copy(
            src_ref=d0.at[h], dst_ref=gv.at[heads + h],
            send_sem=r0_send.at[h], recv_sem=g_sem.at[heads + h],
            device_id={"section": before}, device_id_type=MESH,
        )

    def relay1(h):
        return pltpu.make_async_remote_copy(
            src_ref=d1.at[h], dst_ref=next_hbm.at[0, :, columns(h)],
            send_sem=r1_send.at[h], recv_sem=r1_recv.at[h],
            device_id={"section": before}, device_id_type=MESH,
        )

    def zero_copy(h):
        return pltpu.make_async_copy(
            qo.at[0], next_hbm.at[0, :, columns(h)], r1_recv.at[h]
        )

    def exchange(j):
        return pltpu.make_async_remote_copy(
            src_ref=xs.at[partner(STEPS[j], 1)], dst_ref=xr.at[me],
            send_sem=a2a_send.at[j], recv_sem=a2a_recv.at[j],
            device_id={"tensor": partner(STEPS[j], 1)}, device_id_type=MESH,
        )

    def arrival(j):
        return pltpu.make_async_remote_copy(
            src_ref=xs.at[me], dst_ref=xr.at[partner(STEPS[j], -1)],
            send_sem=a2a_send.at[j], recv_sem=a2a_recv.at[j],
            device_id={"tensor": partner(STEPS[j], 1)}, device_id_type=MESH,
        )

    def q_out(m, h):
        i = m * heads + h
        return pltpu.make_async_copy(qo.at[i], qg_hbm.at[0, m, :, columns(h)], qo_sem.at[i])

    def k_out(m, h):
        i = m * heads + h
        return pltpu.make_async_copy(ko.at[i], kg_hbm.at[0, m, :, columns(h)], ko_sem.at[i])

    barrier = pltpu.get_barrier_semaphore()
    for step in STEPS:
        pl.semaphore_signal(
            barrier, inc=1, device_id={"tensor": partner(step, 1)}, device_id_type=MESH
        )
    for other in (before, after):
        pl.semaphore_signal(
            barrier, inc=1, device_id={"section": other}, device_id_type=MESH
        )

    x_copy = pltpu.make_async_copy(x_hbm.at[0], xv, x_sem)
    s_copy = pltpu.make_async_copy(s_hbm.at[0], sv, s_sem)
    s_copy.start()
    x_copy.start()
    for h in range(heads):
        q_copy(0, h).start()
        k_copy(0, h).start()
        g_copy(h).start()
    for h in range(heads):
        q_copy(1, h).start()
        k_copy(1, h).start()

    @pl.when(is_last)
    def _():
        for h in range(heads):
            loss_copy(h).start()

    s_copy.wait()
    x_copy.wait()
    for m in range(2):
        scales = sv[m].astype(jnp.float32)
        for p in range(8):
            for h in range(heads):
                c = p * heads + h
                wide = xv[m, :, c * HD:(c + 1) * HD].astype(jnp.float32) * scales[:, c:c + 1]
                xs[p, m * heads + h] = wide.astype(jnp.bfloat16)

    pl.semaphore_wait(barrier, len(STEPS) + 2)
    for j in range(len(STEPS)):
        exchange(j).start()
    own_copy = pltpu.make_async_copy(xs.at[me], xr.at[me], own_sem)
    own_copy.start()

    causal = lax.broadcasted_iota(jnp.int32, (tokens, tokens), 1) >= lax.broadcasted_iota(
        jnp.int32, (tokens, tokens), 0
    )

    def weigh(i):
        scores = across(kv[i], qv[i], ((1,), (1,)))
        scores = jnp.where(causal, scores, -1e30)
        scores = scores - jnp.max(scores, axis=0, keepdims=True)
        expon = jnp.exp2(scores * EXP2_SCALE)
        weights = expon * (1.0 / jnp.sum(expon, axis=0, keepdims=True))
        w[i] = weights
        return weights

    def carry(weights, i):
        upstream = gv[i]
        carried = across(weights.astype(jnp.bfloat16), upstream, ((1,), (0,)))
        return (upstream.astype(jnp.float32) + carried).astype(jnp.bfloat16)

    def send_if(condition, copy):
        @pl.when(condition)
        def _():
            copy.start()

    @pl.loop(0, heads)
    def _(h):
        q_copy(0, h).wait()
        k_copy(0, h).wait()
        g_copy(h).wait()
        d0[h] = carry(weigh(h), h)
        send_if((h > 0) & (section > 0), relay0(jnp.maximum(h - 1, 0)))

    @pl.loop(0, heads)
    def _(h):
        q_copy(1, h).wait()
        k_copy(1, h).wait()
        weigh(heads + h)
        send_if((h == 0) & (section > 0), relay0(heads - 1))

    @pl.loop(0, heads)
    def _(h):
        relay0(h).wait_recv()
        d1[h] = carry(w[heads + h], heads + h)
        send_if((h > 0) & (section > 0), relay1(jnp.maximum(h - 1, 0)))

    own_copy.wait()
    for j in range(len(STEPS)):
        arrival(j).wait_recv()
    send_if(section > 0, relay1(heads - 1))

    @pl.loop(0, both)
    def _(i):
        weights, upstream = w[i], gv[i]
        inputs = xr[:, i].reshape(tokens, HD)
        product = across(inputs, upstream, ((1,), (1,)))
        centre = jnp.sum(weights * product, axis=0, keepdims=True)
        diff = (weights * (product - centre)).astype(jnp.bfloat16)
        ko[i] = (across(diff, qv[i], ((1,), (0,))) * SCALING).astype(jnp.bfloat16)
        qo[i] = (across(diff, kv[i], ((0,), (0,))) * SCALING).astype(jnp.bfloat16)

        @pl.when(i > 0)
        def _():
            n = jnp.maximum(i - 1, 0)
            q_out(n // heads, n % heads).start()
            k_out(n // heads, n % heads).start()

    @pl.when(section > 0)
    def _():
        for h in range(heads):
            relay0(h).wait_send()
            relay1(h).wait_send()

    q_out(1, heads - 1).start()
    k_out(1, heads - 1).start()
    for j in range(len(STEPS)):
        exchange(j).wait_send()
    for i in range(both):
        q_out(i // heads, i % heads).wait()
        k_out(i // heads, i % heads).wait()

    @pl.when(is_last)
    def _():
        qo[0] = jnp.zeros((tokens, HD), jnp.bfloat16)
        for h in range(heads):
            zero_copy(h).start()

    for h in range(heads):
        relay1(h).wait_recv()


def solution(mesh):
    sections = mesh.shape["section"]

    def local(grad_in, loss_grad, queries, attn_keys, stored_input, block_scales):
        tokens, width = loss_grad.shape
        heads = width // HD
        rows = stored_input.shape[2]
        both = 2 * heads
        parts = len(STEPS) + 1
        bf16, dma = jnp.bfloat16, pltpu.SemaphoreType.DMA
        anywhere = pl.BlockSpec(memory_space=pl.ANY)
        piece = (tokens, HD)
        return pl.pallas_call(
            functools.partial(kernel, sections, heads),
            out_shape=(
                jax.ShapeDtypeStruct(grad_in.shape, bf16),
                jax.ShapeDtypeStruct(queries.shape, bf16),
                jax.ShapeDtypeStruct(attn_keys.shape, bf16),
            ),
            in_specs=[anywhere] * 6,
            out_specs=(anywhere,) * 3,
            scratch_shapes=[
                pltpu.VMEM(stored_input.shape[1:], bf16),
                pltpu.VMEM(block_scales.shape[1:], bf16),
                pltpu.VMEM((both, *piece), bf16),
                pltpu.VMEM((both, *piece), bf16),
                pltpu.VMEM((both, *piece), bf16),
                pltpu.VMEM((parts, both, rows, HD), bf16),
                pltpu.VMEM((parts, both, rows, HD), bf16),
                pltpu.VMEM((both, tokens, tokens), jnp.float32),
                pltpu.VMEM((heads, *piece), bf16),
                pltpu.VMEM((heads, *piece), bf16),
                pltpu.VMEM((both, *piece), bf16),
                pltpu.VMEM((both, *piece), bf16),
                dma, dma, dma((both,)), dma((both,)), dma((both,)), dma,
                dma((len(STEPS),)), dma((len(STEPS),)),
                dma((heads,)), dma((heads,)), dma((heads,)),
                dma((both,)), dma((both,)),
            ],
            compiler_params=pltpu.CompilerParams(collective_id=0, has_side_effects=True),
            name="relay_attention",
        )(grad_in, loss_grad, queries, attn_keys, stored_input, block_scales)

    return jax.shard_map(
        local,
        mesh=mesh,
        in_specs=(
            P("section", None, "tensor"),
            P(None, "tensor"),
            P("section", None, None, "tensor"),
            P("section", None, None, "tensor"),
            P("section", None, "tensor", None),
            P("section", None, "tensor", None),
        ),
        out_specs=(
            P("section", None, "tensor"),
            P("section", None, None, "tensor"),
            P("section", None, None, "tensor"),
        ),
        check_vma=False,
    )
```

```python
import functools
import math

import jax
import jax.numpy as jnp
from jax import lax
from jax.experimental import pallas as pl
from jax.experimental.pallas import tpu as pltpu
from jax.sharding import PartitionSpec as P

HD = 128
SCALING = 1.0 / math.sqrt(HD)
EXP2_SCALE = SCALING * math.log2(math.e)
MESH = pl.DeviceIdType.MESH
STEPS = ((0, 1), (1, 1), (3, 1), (2, 1), (1, 0), (3, 0), (2, 0))


def across(a, b, dims):
    return lax.dot_general(a, b, (dims, ((), ())), preferred_element_type=jnp.float32)


def kernel(
    sections, heads,
    g_hbm, loss_hbm, q_hbm, k_hbm, x_hbm, s_hbm,
    landed, qo, ko,
    xv, sv, gv, qv, kv, xs, xr, w, d0, d1,
    x_sem, s_sem, g_sem, q_sem, k_sem, own_sem, a2a_send, a2a_recv,
    r0_send, r1_send, r1_recv,
):
    section = lax.axis_index("section")
    me = lax.axis_index("tensor")
    x_me, y_me = me // 2, me % 2
    tokens = gv.shape[1]
    before = (section + sections - 1) % sections
    after = (section + 1) % sections
    is_last = section == sections - 1
    both = 2 * heads

    def partner(step, sign):
        dx, dy = step
        return ((x_me + 4 + sign * dx) % 4) * 2 + (y_me + dy) % 2

    def columns(h):
        return pl.ds(pl.multiple_of(h * HD, HD), HD)

    def q_copy(m, h):
        i = m * heads + h
        return pltpu.make_async_copy(q_hbm.at[0, m, :, columns(h)], qv.at[i], q_sem.at[i])

    def k_copy(m, h):
        i = m * heads + h
        return pltpu.make_async_copy(k_hbm.at[0, m, :, columns(h)], kv.at[i], k_sem.at[i])

    def g_copy(h):
        return pltpu.make_async_copy(g_hbm.at[0, :, columns(h)], gv.at[h], g_sem.at[h])

    def loss_copy(h):
        return pltpu.make_async_copy(
            loss_hbm.at[:, columns(h)], gv.at[heads + h], g_sem.at[heads + h]
        )

    def relay0(h):
        return pltpu.make_async_remote_copy(
            src_ref=d0.at[h], dst_ref=gv.at[heads + h],
            send_sem=r0_send.at[h], recv_sem=g_sem.at[heads + h],
            device_id={"section": before}, device_id_type=MESH,
        )

    def relay1(h):
        return pltpu.make_async_remote_copy(
            src_ref=d1.at[h], dst_ref=landed.at[h],
            send_sem=r1_send.at[h], recv_sem=r1_recv.at[h],
            device_id={"section": before}, device_id_type=MESH,
        )

    def exchange(j):
        return pltpu.make_async_remote_copy(
            src_ref=xs.at[partner(STEPS[j], 1)], dst_ref=xr.at[me],
            send_sem=a2a_send.at[j], recv_sem=a2a_recv.at[j],
            device_id={"tensor": partner(STEPS[j], 1)}, device_id_type=MESH,
        )

    def arrival(j):
        return pltpu.make_async_remote_copy(
            src_ref=xs.at[me], dst_ref=xr.at[partner(STEPS[j], -1)],
            send_sem=a2a_send.at[j], recv_sem=a2a_recv.at[j],
            device_id={"tensor": partner(STEPS[j], 1)}, device_id_type=MESH,
        )

    barrier = pltpu.get_barrier_semaphore()
    for step in STEPS:
        pl.semaphore_signal(
            barrier, inc=1, device_id={"tensor": partner(step, 1)}, device_id_type=MESH
        )
    for other in (before, after):
        pl.semaphore_signal(
            barrier, inc=1, device_id={"section": other}, device_id_type=MESH
        )

    x_copy = pltpu.make_async_copy(x_hbm.at[0], xv, x_sem)
    s_copy = pltpu.make_async_copy(s_hbm.at[0], sv, s_sem)
    s_copy.start()
    x_copy.start()
    for h in range(heads):
        q_copy(0, h).start()
        k_copy(0, h).start()
        g_copy(h).start()
    for h in range(heads):
        q_copy(1, h).start()
        k_copy(1, h).start()

    @pl.when(is_last)
    def _():
        for h in range(heads):
            loss_copy(h).start()

    s_copy.wait()
    x_copy.wait()
    for m in range(2):
        scales = sv[m].astype(jnp.float32)
        for p in range(8):
            for h in range(heads):
                c = p * heads + h
                wide = xv[m, :, c * HD:(c + 1) * HD].astype(jnp.float32) * scales[:, c:c + 1]
                xs[p, m * heads + h] = wide.astype(jnp.bfloat16)

    pl.semaphore_wait(barrier, len(STEPS) + 2)
    for j in range(len(STEPS)):
        exchange(j).start()
    own_copy = pltpu.make_async_copy(xs.at[me], xr.at[me], own_sem)
    own_copy.start()

    causal = lax.broadcasted_iota(jnp.int32, (tokens, tokens), 1) >= lax.broadcasted_iota(
        jnp.int32, (tokens, tokens), 0
    )

    def weigh(i):
        scores = across(kv[i], qv[i], ((1,), (1,)))
        scores = jnp.where(causal, scores, -1e30)
        scores = scores - jnp.max(scores, axis=0, keepdims=True)
        expon = jnp.exp2(scores * EXP2_SCALE)
        weights = expon * (1.0 / jnp.sum(expon, axis=0, keepdims=True))
        w[i] = weights
        return weights

    def carry(weights, i):
        upstream = gv[i]
        carried = across(weights.astype(jnp.bfloat16), upstream, ((1,), (0,)))
        return (upstream.astype(jnp.float32) + carried).astype(jnp.bfloat16)

    def send_if(condition, copy):
        @pl.when(condition)
        def _():
            copy.start()

    @pl.loop(0, heads)
    def _(h):
        q_copy(0, h).wait()
        k_copy(0, h).wait()
        g_copy(h).wait()
        d0[h] = carry(weigh(h), h)
        send_if((h > 0) & (section > 0), relay0(jnp.maximum(h - 1, 0)))

    @pl.loop(0, heads)
    def _(h):
        q_copy(1, h).wait()
        k_copy(1, h).wait()
        weigh(heads + h)
        send_if((h == 0) & (section > 0), relay0(heads - 1))

    @pl.loop(0, heads)
    def _(h):
        relay0(h).wait_recv()
        d1[h] = carry(w[heads + h], heads + h)
        send_if((h > 0) & (section > 0), relay1(jnp.maximum(h - 1, 0)))

    own_copy.wait()
    for j in range(len(STEPS)):
        arrival(j).wait_recv()
    send_if(section > 0, relay1(heads - 1))

    @pl.loop(0, both)
    def _(i):
        weights, upstream = w[i], gv[i]
        inputs = xr[:, i].reshape(tokens, HD)
        product = across(inputs, upstream, ((1,), (1,)))
        centre = jnp.sum(weights * product, axis=0, keepdims=True)
        diff = (weights * (product - centre)).astype(jnp.bfloat16)
        ko[i] = (across(diff, qv[i], ((1,), (0,))) * SCALING).astype(jnp.bfloat16)
        qo[i] = (across(diff, kv[i], ((0,), (0,))) * SCALING).astype(jnp.bfloat16)

    @pl.when(section > 0)
    def _():
        for h in range(heads):
            relay0(h).wait_send()
            relay1(h).wait_send()

    for j in range(len(STEPS)):
        exchange(j).wait_send()

    @pl.when(jnp.logical_not(is_last))
    def _():
        for h in range(heads):
            relay1(h).wait_recv()

    @pl.when(is_last)
    def _():
        landed[...] = jnp.zeros_like(landed)


def place(heads, landed, qo, ko, next_hbm, qg_hbm, kg_hbm, next_sem, q_sem, k_sem):
    copies = []
    for i in range(2 * heads):
        m, h = divmod(i, heads)
        cols = pl.ds(h * HD, HD)
        copies.append(pltpu.make_async_copy(qo.at[i], qg_hbm.at[0, m, :, cols], q_sem.at[i]))
        copies.append(pltpu.make_async_copy(ko.at[i], kg_hbm.at[0, m, :, cols], k_sem.at[i]))
        if m == 0:
            copies.append(
                pltpu.make_async_copy(landed.at[h], next_hbm.at[0, :, cols], next_sem.at[h])
            )
    for copy in copies:
        copy.start()
    for copy in copies:
        copy.wait()


def solution(mesh):
    sections = mesh.shape["section"]

    def local(*arguments):
        grad_in, loss_grad, queries, attn_keys, stored_input, block_scales = arguments
        tokens, width = loss_grad.shape
        heads = width // HD
        rows = stored_input.shape[2]
        both = 2 * heads
        parts = len(STEPS) + 1
        bf16, dma = jnp.bfloat16, pltpu.SemaphoreType.DMA
        anywhere = pl.BlockSpec(memory_space=pltpu.HBM)
        piece = (tokens, HD)
        inside = pl.BlockSpec(memory_space=pltpu.VMEM)
        held = pl.pallas_call(
            functools.partial(kernel, sections, heads),
            out_shape=(
                jax.ShapeDtypeStruct((heads, *piece), bf16),
                jax.ShapeDtypeStruct((both, *piece), bf16),
                jax.ShapeDtypeStruct((both, *piece), bf16),
            ),
            in_specs=[anywhere] * 6,
            out_specs=(inside,) * 3,
            scratch_shapes=[
                pltpu.VMEM(stored_input.shape[1:], bf16),
                pltpu.VMEM(block_scales.shape[1:], bf16),
                pltpu.VMEM((both, *piece), bf16),
                pltpu.VMEM((both, *piece), bf16),
                pltpu.VMEM((both, *piece), bf16),
                pltpu.VMEM((parts, both, rows, HD), bf16),
                pltpu.VMEM((parts, both, rows, HD), bf16),
                pltpu.VMEM((both, tokens, tokens), jnp.float32),
                pltpu.VMEM((heads, *piece), bf16),
                pltpu.VMEM((heads, *piece), bf16),
                dma, dma, dma((both,)), dma((both,)), dma((both,)), dma,
                dma((len(STEPS),)), dma((len(STEPS),)),
                dma((heads,)), dma((heads,)), dma((heads,)),
            ],
            compiler_params=pltpu.CompilerParams(
                collective_id=0, has_side_effects=True, vmem_limit_bytes=24 * 2**20
            ),
            name="relay_attention",
        )(*(pltpu.with_memory_space_constraint(a, pltpu.HBM) for a in arguments))
        return pl.pallas_call(
            functools.partial(place, heads),
            out_shape=(
                jax.ShapeDtypeStruct(grad_in.shape, bf16),
                jax.ShapeDtypeStruct(queries.shape, bf16),
                jax.ShapeDtypeStruct(attn_keys.shape, bf16),
            ),
            in_specs=[inside] * 3,
            out_specs=(anywhere,) * 3,
            scratch_shapes=[dma((heads,)), dma((both,)), dma((both,))],
            compiler_params=pltpu.CompilerParams(vmem_limit_bytes=8 * 2**20),
            name="place",
        )(*held)

    return jax.shard_map(
        local,
        mesh=mesh,
        in_specs=(
            P("section", None, "tensor"),
            P(None, "tensor"),
            P("section", None, None, "tensor"),
            P("section", None, None, "tensor"),
            P("section", None, "tensor", None),
            P("section", None, "tensor", None),
        ),
        out_specs=(
            P("section", None, "tensor"),
            P("section", None, None, "tensor"),
            P("section", None, None, "tensor"),
        ),
        check_vma=False,
    )
```

```python
import functools
import math

import jax
import jax.numpy as jnp
from jax import lax
from jax.experimental import pallas as pl
from jax.experimental.pallas import tpu as pltpu
from jax.sharding import PartitionSpec as P

HD = 128
SCALING = 1.0 / math.sqrt(HD)
EXP2_SCALE = SCALING * math.log2(math.e)
PAIR = 2
MESH = pl.DeviceIdType.MESH
STEPS = ((0, 1), (1, 1), (3, 1), (2, 1), (1, 0), (3, 0), (2, 0))


def across(a, b, dims):
    return lax.dot_general(a, b, (dims, ((), ())), preferred_element_type=jnp.float32)


def kernel(
    sections, heads,
    g_hbm, loss_hbm, q_hbm, k_hbm, x_hbm, s_hbm,
    landed, qo, ko,
    xv, sv, gv, qv, kv, xs, xr, w, d0, d1,
    x_sem, s_sem, g_sem, q_sem, k_sem, own_sem, a2a_send, a2a_recv,
    r0_send, r1_send, r1_recv,
):
    section = lax.axis_index("section")
    me = lax.axis_index("tensor")
    x_me, y_me = me // 2, me % 2
    tokens = gv.shape[1]
    before = (section + sections - 1) % sections
    after = (section + 1) % sections
    is_last = section == sections - 1
    both = 2 * heads

    def partner(step, sign):
        dx, dy = step
        return ((x_me + 4 + sign * dx) % 4) * 2 + (y_me + dy) % 2

    def columns(h):
        return pl.ds(pl.multiple_of(h * HD, HD), HD)

    def q_copy(m, h):
        i = m * heads + h
        return pltpu.make_async_copy(q_hbm.at[0, m, :, columns(h)], qv.at[i], q_sem.at[i])

    def k_copy(m, h):
        i = m * heads + h
        return pltpu.make_async_copy(k_hbm.at[0, m, :, columns(h)], kv.at[i], k_sem.at[i])

    def g_copy(h):
        return pltpu.make_async_copy(g_hbm.at[0, :, columns(h)], gv.at[h], g_sem.at[h])

    def loss_copy(h):
        return pltpu.make_async_copy(
            loss_hbm.at[:, columns(h)], gv.at[heads + h], g_sem.at[heads + h]
        )

    def relay0(h):
        return pltpu.make_async_remote_copy(
            src_ref=d0.at[h], dst_ref=gv.at[heads + h],
            send_sem=r0_send.at[h], recv_sem=g_sem.at[heads + h],
            device_id={"section": before}, device_id_type=MESH,
        )

    def relay1(h):
        return pltpu.make_async_remote_copy(
            src_ref=d1.at[h], dst_ref=landed.at[h],
            send_sem=r1_send.at[h], recv_sem=r1_recv.at[h],
            device_id={"section": before}, device_id_type=MESH,
        )

    def exchange(j):
        return pltpu.make_async_remote_copy(
            src_ref=xs.at[partner(STEPS[j], 1)], dst_ref=xr.at[me],
            send_sem=a2a_send.at[j], recv_sem=a2a_recv.at[j],
            device_id={"tensor": partner(STEPS[j], 1)}, device_id_type=MESH,
        )

    def arrival(j):
        return pltpu.make_async_remote_copy(
            src_ref=xs.at[me], dst_ref=xr.at[partner(STEPS[j], -1)],
            send_sem=a2a_send.at[j], recv_sem=a2a_recv.at[j],
            device_id={"tensor": partner(STEPS[j], 1)}, device_id_type=MESH,
        )

    barrier = pltpu.get_barrier_semaphore()
    for step in STEPS:
        pl.semaphore_signal(
            barrier, inc=1, device_id={"tensor": partner(step, 1)}, device_id_type=MESH
        )
    for other in (before, after):
        pl.semaphore_signal(
            barrier, inc=1, device_id={"section": other}, device_id_type=MESH
        )

    x_copy = pltpu.make_async_copy(x_hbm.at[0], xv, x_sem)
    s_copy = pltpu.make_async_copy(s_hbm.at[0], sv, s_sem)
    s_copy.start()
    x_copy.start()
    for h in range(heads):
        q_copy(0, h).start()
        k_copy(0, h).start()
        g_copy(h).start()
    for h in range(heads):
        q_copy(1, h).start()
        k_copy(1, h).start()

    @pl.when(is_last)
    def _():
        for h in range(heads):
            loss_copy(h).start()

    s_copy.wait()
    x_copy.wait()
    for m in range(2):
        scales = sv[m].astype(jnp.float32)
        for p in range(8):
            for h in range(heads):
                c = p * heads + h
                wide = xv[m, :, c * HD:(c + 1) * HD].astype(jnp.float32) * scales[:, c:c + 1]
                xs[p, m * heads + h] = wide.astype(jnp.bfloat16)

    pl.semaphore_wait(barrier, len(STEPS) + 2)
    for j in range(len(STEPS)):
        exchange(j).start()
    own_copy = pltpu.make_async_copy(xs.at[me], xr.at[me], own_sem)
    own_copy.start()

    causal = lax.broadcasted_iota(jnp.int32, (tokens, tokens), 1) >= lax.broadcasted_iota(
        jnp.int32, (tokens, tokens), 0
    )

    def weigh(keys, queries):
        scores = across(keys, queries, ((1,), (1,)))
        scores = jnp.where(causal, scores, -1e30)
        scores = scores - jnp.max(scores, axis=0, keepdims=True)
        expon = jnp.exp2(scores * EXP2_SCALE)
        return expon * (1.0 / jnp.sum(expon, axis=0, keepdims=True))

    def carry(weights, upstream):
        carried = across(weights.astype(jnp.bfloat16), upstream, ((1,), (0,)))
        return (upstream.astype(jnp.float32) + carried).astype(jnp.bfloat16)

    def score_grads(weights, upstream, inputs, queries, keys):
        product = across(inputs, upstream, ((1,), (1,)))
        centre = jnp.sum(weights * product, axis=0, keepdims=True)
        diff = (weights * (product - centre)).astype(jnp.bfloat16)
        for_keys = across(diff, queries, ((1,), (0,))) * SCALING
        for_queries = across(diff, keys, ((0,), (0,))) * SCALING
        return for_queries.astype(jnp.bfloat16), for_keys.astype(jnp.bfloat16)

    def send_if(condition, relay, n):
        @pl.when(condition)
        def _():
            for h in range(PAIR):
                relay(n * PAIR + h).start()

    def group(n):
        return [n * PAIR + h for h in range(PAIR)]

    steps = heads // PAIR

    @pl.loop(0, steps)
    def _(n):
        for h in group(n):
            q_copy(0, h).wait()
            k_copy(0, h).wait()
            g_copy(h).wait()
            q_copy(1, h).wait()
            k_copy(1, h).wait()
        here = group(n) + [heads + h for h in group(n)]
        loaded = [(kv[i], qv[i]) for i in here]
        upstream = [gv[h] for h in group(n)]
        weights = [weigh(*pair) for pair in loaded]
        carried = [carry(*pair) for pair in zip(weights, upstream)]
        for h, value in zip(group(n), carried):
            d0[h] = value
        for i, value in zip(here, weights):
            w[i] = value
        send_if((n > 0) & (section > 0), relay0, jnp.maximum(n - 1, 0))

    @pl.loop(0, steps)
    def _(n):
        send_if((n == 0) & (section > 0), relay0, steps - 1)
        for h in group(n):
            relay0(h).wait_recv()
        loaded = [(w[heads + h], gv[heads + h]) for h in group(n)]
        carried = [carry(*pair) for pair in loaded]
        for h, value in zip(group(n), carried):
            d1[h] = value
        send_if((n > 0) & (section > 0), relay1, jnp.maximum(n - 1, 0))

    own_copy.wait()
    for j in range(len(STEPS)):
        arrival(j).wait_recv()
    send_if(section > 0, relay1, steps - 1)

    @pl.loop(0, 2 * steps)
    def _(n):
        loaded = [
            (w[i], gv[i], xr[:, i].reshape(tokens, HD), qv[i], kv[i]) for i in group(n)
        ]
        results = [score_grads(*values) for values in loaded]
        for i, (for_queries, for_keys) in zip(group(n), results):
            qo[i] = for_queries
            ko[i] = for_keys

    @pl.when(section > 0)
    def _():
        for h in range(heads):
            relay0(h).wait_send()
            relay1(h).wait_send()

    for j in range(len(STEPS)):
        exchange(j).wait_send()

    @pl.when(jnp.logical_not(is_last))
    def _():
        for h in range(heads):
            relay1(h).wait_recv()

    @pl.when(is_last)
    def _():
        landed[...] = jnp.zeros_like(landed)


def place(heads, landed, qo, ko, next_hbm, qg_hbm, kg_hbm, next_sem, q_sem, k_sem):
    copies = []
    for i in range(2 * heads):
        m, h = divmod(i, heads)
        cols = pl.ds(h * HD, HD)
        copies.append(pltpu.make_async_copy(qo.at[i], qg_hbm.at[0, m, :, cols], q_sem.at[i]))
        copies.append(pltpu.make_async_copy(ko.at[i], kg_hbm.at[0, m, :, cols], k_sem.at[i]))
        if m == 0:
            copies.append(
                pltpu.make_async_copy(landed.at[h], next_hbm.at[0, :, cols], next_sem.at[h])
            )
    for copy in copies:
        copy.start()
    for copy in copies:
        copy.wait()


def solution(mesh):
    sections = mesh.shape["section"]

    def local(*arguments):
        grad_in, loss_grad, queries, attn_keys, stored_input, block_scales = arguments
        tokens, width = loss_grad.shape
        heads = width // HD
        rows = stored_input.shape[2]
        both = 2 * heads
        parts = len(STEPS) + 1
        bf16, dma = jnp.bfloat16, pltpu.SemaphoreType.DMA
        anywhere = pl.BlockSpec(memory_space=pltpu.HBM)
        piece = (tokens, HD)
        inside = pl.BlockSpec(memory_space=pltpu.VMEM)
        held = pl.pallas_call(
            functools.partial(kernel, sections, heads),
            out_shape=(
                jax.ShapeDtypeStruct((heads, *piece), bf16),
                jax.ShapeDtypeStruct((both, *piece), bf16),
                jax.ShapeDtypeStruct((both, *piece), bf16),
            ),
            in_specs=[anywhere] * 6,
            out_specs=(inside,) * 3,
            scratch_shapes=[
                pltpu.VMEM(stored_input.shape[1:], bf16),
                pltpu.VMEM(block_scales.shape[1:], bf16),
                pltpu.VMEM((both, *piece), bf16),
                pltpu.VMEM((both, *piece), bf16),
                pltpu.VMEM((both, *piece), bf16),
                pltpu.VMEM((parts, both, rows, HD), bf16),
                pltpu.VMEM((parts, both, rows, HD), bf16),
                pltpu.VMEM((both, tokens, tokens), jnp.float32),
                pltpu.VMEM((heads, *piece), bf16),
                pltpu.VMEM((heads, *piece), bf16),
                dma, dma, dma((both,)), dma((both,)), dma((both,)), dma,
                dma((len(STEPS),)), dma((len(STEPS),)),
                dma((heads,)), dma((heads,)), dma((heads,)),
            ],
            compiler_params=pltpu.CompilerParams(
                collective_id=0, has_side_effects=True, vmem_limit_bytes=24 * 2**20
            ),
            name="relay_attention",
        )(*(pltpu.with_memory_space_constraint(a, pltpu.HBM) for a in arguments))
        return pl.pallas_call(
            functools.partial(place, heads),
            out_shape=(
                jax.ShapeDtypeStruct(grad_in.shape, bf16),
                jax.ShapeDtypeStruct(queries.shape, bf16),
                jax.ShapeDtypeStruct(attn_keys.shape, bf16),
            ),
            in_specs=[inside] * 3,
            out_specs=(anywhere,) * 3,
            scratch_shapes=[dma((heads,)), dma((both,)), dma((both,))],
            compiler_params=pltpu.CompilerParams(vmem_limit_bytes=8 * 2**20),
            name="place",
        )(*held)

    return jax.shard_map(
        local,
        mesh=mesh,
        in_specs=(
            P("section", None, "tensor"),
            P(None, "tensor"),
            P("section", None, None, "tensor"),
            P("section", None, None, "tensor"),
            P("section", None, "tensor", None),
            P("section", None, "tensor", None),
        ),
        out_specs=(
            P("section", None, "tensor"),
            P("section", None, None, "tensor"),
            P("section", None, None, "tensor"),
        ),
        check_vma=False,
    )
```

```python
import functools
import math

import jax
import jax.numpy as jnp
from jax import lax
from jax.experimental import pallas as pl
from jax.experimental.pallas import tpu as pltpu
from jax.sharding import PartitionSpec as P

HD = 128
SCALING = 1.0 / math.sqrt(HD)
EXP2_SCALE = SCALING * math.log2(math.e)
PAIR = 2
MESH = pl.DeviceIdType.MESH
STEPS = ((0, 1), (1, 1), (3, 1), (2, 1), (1, 0), (3, 0), (2, 0))


def across(a, b, dims):
    return lax.dot_general(a, b, (dims, ((), ())), preferred_element_type=jnp.float32)


def kernel(
    sections, heads,
    g_hbm, loss_hbm, q_hbm, k_hbm, x_hbm, s_hbm,
    landed, qo, ko,
    xv, sv, gv, qv, kv, xs, xr, w, d0, d1,
    x_sem, s_sem, g_sem, q_sem, k_sem, own_sem, a2a_send, a2a_recv,
    r0_send, r1_send, r1_recv,
):
    section = lax.axis_index("section")
    me = lax.axis_index("tensor")
    x_me, y_me = me // 2, me % 2
    tokens = gv.shape[1]
    before = (section + sections - 1) % sections
    after = (section + 1) % sections
    is_last = section == sections - 1
    both = 2 * heads

    def partner(step, sign):
        dx, dy = step
        return ((x_me + 4 + sign * dx) % 4) * 2 + (y_me + dy) % 2

    def columns(h):
        return pl.ds(pl.multiple_of(h * HD, HD), HD)

    def q_copy(m, h):
        i = m * heads + h
        return pltpu.make_async_copy(q_hbm.at[0, m, :, columns(h)], qv.at[i], q_sem.at[i])

    def k_copy(m, h):
        i = m * heads + h
        return pltpu.make_async_copy(k_hbm.at[0, m, :, columns(h)], kv.at[i], k_sem.at[i])

    def g_copy(h):
        return pltpu.make_async_copy(g_hbm.at[0, :, columns(h)], gv.at[h], g_sem.at[h])

    def loss_copy(h):
        return pltpu.make_async_copy(
            loss_hbm.at[:, columns(h)], gv.at[heads + h], g_sem.at[heads + h]
        )

    def relay0(h):
        return pltpu.make_async_remote_copy(
            src_ref=d0.at[h], dst_ref=gv.at[heads + h],
            send_sem=r0_send.at[h], recv_sem=g_sem.at[heads + h],
            device_id={"section": before}, device_id_type=MESH,
        )

    def relay1(h):
        return pltpu.make_async_remote_copy(
            src_ref=d1.at[h], dst_ref=landed.at[h],
            send_sem=r1_send.at[h], recv_sem=r1_recv.at[h],
            device_id={"section": before}, device_id_type=MESH,
        )

    def exchange(j):
        return pltpu.make_async_remote_copy(
            src_ref=xs.at[partner(STEPS[j], 1)], dst_ref=xr.at[me],
            send_sem=a2a_send.at[j], recv_sem=a2a_recv.at[j],
            device_id={"tensor": partner(STEPS[j], 1)}, device_id_type=MESH,
        )

    def arrival(j):
        return pltpu.make_async_remote_copy(
            src_ref=xs.at[me], dst_ref=xr.at[partner(STEPS[j], -1)],
            send_sem=a2a_send.at[j], recv_sem=a2a_recv.at[j],
            device_id={"tensor": partner(STEPS[j], 1)}, device_id_type=MESH,
        )

    barrier = pltpu.get_barrier_semaphore()
    for step in STEPS:
        pl.semaphore_signal(
            barrier, inc=1, device_id={"tensor": partner(step, 1)}, device_id_type=MESH
        )
    for other in (before, after):
        pl.semaphore_signal(
            barrier, inc=1, device_id={"section": other}, device_id_type=MESH
        )

    x_copy = pltpu.make_async_copy(x_hbm.at[0], xv, x_sem)
    s_copy = pltpu.make_async_copy(s_hbm.at[0], sv, s_sem)
    s_copy.start()
    x_copy.start()
    for h in range(heads):
        q_copy(0, h).start()
        k_copy(0, h).start()
        g_copy(h).start()
    for h in range(heads):
        q_copy(1, h).start()
        k_copy(1, h).start()

    @pl.when(is_last)
    def _():
        for h in range(heads):
            loss_copy(h).start()

    s_copy.wait()
    x_copy.wait()
    for m in range(2):
        scales = sv[m].astype(jnp.float32)
        for p in range(8):
            for h in range(heads):
                c = p * heads + h
                wide = xv[m, :, c * HD:(c + 1) * HD].astype(jnp.float32) * scales[:, c:c + 1]
                xs[p, m * heads + h] = wide.astype(jnp.bfloat16)

    pl.semaphore_wait(barrier, len(STEPS) + 2)
    for j in range(len(STEPS)):
        exchange(j).start()
    own_copy = pltpu.make_async_copy(xs.at[me], xr.at[me], own_sem)
    own_copy.start()

    causal = lax.broadcasted_iota(jnp.int32, (tokens, tokens), 1) >= lax.broadcasted_iota(
        jnp.int32, (tokens, tokens), 0
    )

    def weigh(keys, queries):
        scores = across(keys, queries, ((1,), (1,)))
        scores = jnp.where(causal, scores, -1e30)
        scores = scores - jnp.max(scores, axis=0, keepdims=True)
        expon = jnp.exp2(scores * EXP2_SCALE)
        return expon * (1.0 / jnp.sum(expon, axis=0, keepdims=True))

    def carry(weights, upstream):
        carried = across(weights.astype(jnp.bfloat16), upstream, ((1,), (0,)))
        return (upstream.astype(jnp.float32) + carried).astype(jnp.bfloat16)

    def score_grads(weights, upstream, inputs, queries, keys):
        product = across(inputs, upstream, ((1,), (1,)))
        centre = jnp.sum(weights * product, axis=0, keepdims=True)
        diff = (weights * (product - centre)).astype(jnp.bfloat16)
        for_keys = across(diff, queries, ((1,), (0,))) * SCALING
        for_queries = across(diff, keys, ((0,), (0,))) * SCALING
        return for_queries.astype(jnp.bfloat16), for_keys.astype(jnp.bfloat16)

    def group(n):
        return [n * PAIR + h for h in range(PAIR)]

    steps = heads // PAIR

    @pl.loop(0, steps)
    def _(n):
        for h in group(n):
            q_copy(0, h).wait()
            k_copy(0, h).wait()
            g_copy(h).wait()
            q_copy(1, h).wait()
            k_copy(1, h).wait()
        here = group(n) + [heads + h for h in group(n)]
        loaded = [(kv[i], qv[i]) for i in here]
        upstream = [gv[h] for h in group(n)]
        weights = [weigh(*pair) for pair in loaded]
        carried = [carry(*pair) for pair in zip(weights, upstream)]
        for h, value in zip(group(n), carried):
            d0[h] = value
        for i, value in zip(here, weights):
            w[i] = value
        @pl.when(section > 0)
        def _():
            for h in group(n):
                relay0(h).start()

    @pl.loop(0, heads)
    def _(h):
        relay0(h).wait_recv()
        d1[h] = carry(w[heads + h], gv[heads + h])

        @pl.when(section > 0)
        def _():
            relay1(h).start()

    own_copy.wait()
    for j in range(len(STEPS)):
        arrival(j).wait_recv()

    @pl.loop(0, 2 * steps)
    def _(n):
        loaded = [
            (w[i], gv[i], xr[:, i].reshape(tokens, HD), qv[i], kv[i]) for i in group(n)
        ]
        results = [score_grads(*values) for values in loaded]
        for i, (for_queries, for_keys) in zip(group(n), results):
            qo[i] = for_queries
            ko[i] = for_keys

    @pl.when(section > 0)
    def _():
        for h in range(heads):
            relay0(h).wait_send()
            relay1(h).wait_send()

    for j in range(len(STEPS)):
        exchange(j).wait_send()

    @pl.when(jnp.logical_not(is_last))
    def _():
        for h in range(heads):
            relay1(h).wait_recv()

    @pl.when(is_last)
    def _():
        landed[...] = jnp.zeros_like(landed)


def place(heads, landed, qo, ko, next_hbm, qg_hbm, kg_hbm, next_sem, q_sem, k_sem):
    copies = []
    for i in range(2 * heads):
        m, h = divmod(i, heads)
        cols = pl.ds(h * HD, HD)
        copies.append(pltpu.make_async_copy(qo.at[i], qg_hbm.at[0, m, :, cols], q_sem.at[i]))
        copies.append(pltpu.make_async_copy(ko.at[i], kg_hbm.at[0, m, :, cols], k_sem.at[i]))
        if m == 0:
            copies.append(
                pltpu.make_async_copy(landed.at[h], next_hbm.at[0, :, cols], next_sem.at[h])
            )
    for copy in copies:
        copy.start()
    for copy in copies:
        copy.wait()


def solution(mesh):
    sections = mesh.shape["section"]

    def local(*arguments):
        grad_in, loss_grad, queries, attn_keys, stored_input, block_scales = arguments
        tokens, width = loss_grad.shape
        heads = width // HD
        rows = stored_input.shape[2]
        both = 2 * heads
        parts = len(STEPS) + 1
        bf16, dma = jnp.bfloat16, pltpu.SemaphoreType.DMA
        anywhere = pl.BlockSpec(memory_space=pltpu.HBM)
        piece = (tokens, HD)
        inside = pl.BlockSpec(memory_space=pltpu.VMEM)
        held = pl.pallas_call(
            functools.partial(kernel, sections, heads),
            out_shape=(
                jax.ShapeDtypeStruct((heads, *piece), bf16),
                jax.ShapeDtypeStruct((both, *piece), bf16),
                jax.ShapeDtypeStruct((both, *piece), bf16),
            ),
            in_specs=[anywhere] * 6,
            out_specs=(inside,) * 3,
            scratch_shapes=[
                pltpu.VMEM(stored_input.shape[1:], bf16),
                pltpu.VMEM(block_scales.shape[1:], bf16),
                pltpu.VMEM((both, *piece), bf16),
                pltpu.VMEM((both, *piece), bf16),
                pltpu.VMEM((both, *piece), bf16),
                pltpu.VMEM((parts, both, rows, HD), bf16),
                pltpu.VMEM((parts, both, rows, HD), bf16),
                pltpu.VMEM((both, tokens, tokens), jnp.float32),
                pltpu.VMEM((heads, *piece), bf16),
                pltpu.VMEM((heads, *piece), bf16),
                dma, dma, dma((both,)), dma((both,)), dma((both,)), dma,
                dma((len(STEPS),)), dma((len(STEPS),)),
                dma((heads,)), dma((heads,)), dma((heads,)),
            ],
            compiler_params=pltpu.CompilerParams(
                collective_id=0, has_side_effects=True, vmem_limit_bytes=24 * 2**20
            ),
            name="relay_attention",
        )(*(pltpu.with_memory_space_constraint(a, pltpu.HBM) for a in arguments))
        return pl.pallas_call(
            functools.partial(place, heads),
            out_shape=(
                jax.ShapeDtypeStruct(grad_in.shape, bf16),
                jax.ShapeDtypeStruct(queries.shape, bf16),
                jax.ShapeDtypeStruct(attn_keys.shape, bf16),
            ),
            in_specs=[inside] * 3,
            out_specs=(anywhere,) * 3,
            scratch_shapes=[dma((heads,)), dma((both,)), dma((both,))],
            compiler_params=pltpu.CompilerParams(vmem_limit_bytes=8 * 2**20),
            name="place",
        )(*held)

    return jax.shard_map(
        local,
        mesh=mesh,
        in_specs=(
            P("section", None, "tensor"),
            P(None, "tensor"),
            P("section", None, None, "tensor"),
            P("section", None, None, "tensor"),
            P("section", None, "tensor", None),
            P("section", None, "tensor", None),
        ),
        out_specs=(
            P("section", None, "tensor"),
            P("section", None, None, "tensor"),
            P("section", None, None, "tensor"),
        ),
        check_vma=False,
    )
```

```python
import functools
import math

import jax
import jax.numpy as jnp
from jax import lax
from jax.experimental import pallas as pl
from jax.experimental.pallas import tpu as pltpu
from jax.sharding import PartitionSpec as P

HD = 128
SCALING = 1.0 / math.sqrt(HD)
EXP2_SCALE = SCALING * math.log2(math.e)
PAIR = 2
MESH = pl.DeviceIdType.MESH
STEPS = ((0, 1), (1, 1), (3, 1), (2, 1), (1, 0), (3, 0), (2, 0))


def across(a, b, dims):
    return lax.dot_general(a, b, (dims, ((), ())), preferred_element_type=jnp.float32)


def kernel(
    sections, heads,
    g_hbm, loss_hbm, q_hbm, k_hbm, x_hbm, s_hbm,
    landed, qo, ko,
    xv, sv, gv, qv, kv, xs, xr, w, d0, d1,
    x_sem, s_sem, g_sem, q_sem, k_sem, own_sem, a2a_send, a2a_recv,
    r0_send, r1_send, r1_recv,
):
    section = lax.axis_index("section")
    me = lax.axis_index("tensor")
    x_me, y_me = me // 2, me % 2
    tokens = gv.shape[1]
    before = (section + sections - 1) % sections
    after = (section + 1) % sections
    is_last = section == sections - 1
    both = 2 * heads

    def partner(step, sign):
        dx, dy = step
        return ((x_me + 4 + sign * dx) % 4) * 2 + (y_me + dy) % 2

    def columns(h):
        return pl.ds(pl.multiple_of(h * HD, HD), HD)

    def q_copy(m, h):
        i = m * heads + h
        return pltpu.make_async_copy(q_hbm.at[0, m, :, columns(h)], qv.at[i], q_sem.at[i])

    def k_copy(m, h):
        i = m * heads + h
        return pltpu.make_async_copy(k_hbm.at[0, m, :, columns(h)], kv.at[i], k_sem.at[i])

    def g_copy(h):
        return pltpu.make_async_copy(g_hbm.at[0, :, columns(h)], gv.at[h], g_sem.at[h])

    def loss_copy(h):
        return pltpu.make_async_copy(
            loss_hbm.at[:, columns(h)], gv.at[heads + h], g_sem.at[heads + h]
        )

    def relay0(h):
        return pltpu.make_async_remote_copy(
            src_ref=d0.at[h], dst_ref=gv.at[heads + h],
            send_sem=r0_send.at[h], recv_sem=g_sem.at[heads + h],
            device_id={"section": before}, device_id_type=MESH,
        )

    def relay1(h):
        return pltpu.make_async_remote_copy(
            src_ref=d1.at[h], dst_ref=landed.at[h],
            send_sem=r1_send.at[h], recv_sem=r1_recv.at[h],
            device_id={"section": before}, device_id_type=MESH,
        )

    def exchange(j):
        return pltpu.make_async_remote_copy(
            src_ref=xs.at[partner(STEPS[j], 1)], dst_ref=xr.at[me],
            send_sem=a2a_send.at[j], recv_sem=a2a_recv.at[j],
            device_id={"tensor": partner(STEPS[j], 1)}, device_id_type=MESH,
        )

    def arrival(j):
        return pltpu.make_async_remote_copy(
            src_ref=xs.at[me], dst_ref=xr.at[partner(STEPS[j], -1)],
            send_sem=a2a_send.at[j], recv_sem=a2a_recv.at[j],
            device_id={"tensor": partner(STEPS[j], 1)}, device_id_type=MESH,
        )

    barrier = pltpu.get_barrier_semaphore()
    for step in STEPS:
        pl.semaphore_signal(
            barrier, inc=1, device_id={"tensor": partner(step, 1)}, device_id_type=MESH
        )
    for other in (before, after):
        pl.semaphore_signal(
            barrier, inc=1, device_id={"section": other}, device_id_type=MESH
        )

    x_copy = pltpu.make_async_copy(x_hbm.at[0], xv, x_sem)
    s_copy = pltpu.make_async_copy(s_hbm.at[0], sv, s_sem)
    s_copy.start()
    x_copy.start()
    for h in range(heads):
        q_copy(0, h).start()
        k_copy(0, h).start()
        g_copy(h).start()
    for h in range(heads):
        q_copy(1, h).start()
        k_copy(1, h).start()

    @pl.when(is_last)
    def _():
        for h in range(heads):
            loss_copy(h).start()

    s_copy.wait()
    x_copy.wait()
    for m in range(2):
        scales = sv[m].astype(jnp.float32)
        for p in range(8):
            for h in range(heads):
                c = p * heads + h
                wide = xv[m, :, c * HD:(c + 1) * HD].astype(jnp.float32) * scales[:, c:c + 1]
                xs[p, m * heads + h] = wide.astype(jnp.bfloat16)

    pl.semaphore_wait(barrier, len(STEPS) + 2)
    for j in range(len(STEPS)):
        exchange(j).start()
    own_copy = pltpu.make_async_copy(xs.at[me], xr.at[me], own_sem)
    own_copy.start()

    causal = lax.broadcasted_iota(jnp.int32, (tokens, tokens), 1) >= lax.broadcasted_iota(
        jnp.int32, (tokens, tokens), 0
    )

    def weigh(keys, queries):
        scores = across(keys, queries, ((1,), (1,)))
        scores = jnp.where(causal, scores, -1e30)
        scores = scores - jnp.max(scores, axis=0, keepdims=True)
        expon = jnp.exp2(scores * EXP2_SCALE)
        return expon * (1.0 / jnp.sum(expon, axis=0, keepdims=True))

    def carry(weights, upstream):
        carried = across(weights.astype(jnp.bfloat16), upstream, ((1,), (0,)))
        return (upstream.astype(jnp.float32) + carried).astype(jnp.bfloat16)

    def score_grads(weights, upstream, inputs, queries, keys):
        product = across(inputs, upstream, ((1,), (1,)))
        centre = jnp.sum(weights * product, axis=0, keepdims=True)
        diff = (weights * (product - centre)).astype(jnp.bfloat16)
        for_keys = across(diff, queries, ((1,), (0,))) * SCALING
        for_queries = across(diff, keys, ((0,), (0,))) * SCALING
        return for_queries.astype(jnp.bfloat16), for_keys.astype(jnp.bfloat16)

    def group(n):
        return [n * PAIR + h for h in range(PAIR)]

    steps = heads // PAIR

    @pl.loop(0, steps)
    def _(n):
        for h in group(n):
            q_copy(0, h).wait()
            k_copy(0, h).wait()
            g_copy(h).wait()
            q_copy(1, h).wait()
            k_copy(1, h).wait()
        here = group(n) + [heads + h for h in group(n)]
        loaded = [(kv[i], qv[i]) for i in here]
        upstream = [gv[h] for h in group(n)]
        weights = [weigh(*pair) for pair in loaded]
        carried = [carry(*pair) for pair in zip(weights, upstream)]
        for h, value in zip(group(n), carried):
            d0[h] = value
        for i, value in zip(here, weights):
            w[i] = value
        @pl.when(section > 0)
        def _():
            for h in group(n):
                relay0(h).start()

    @pl.loop(0, heads)
    def _(h):
        relay0(h).wait_recv()
        d1[h] = carry(w[heads + h], gv[heads + h])

        @pl.when(section > 0)
        def _():
            relay1(h).start()

    own_copy.wait()
    for j in range(len(STEPS)):
        arrival(j).wait_recv()

    @pl.loop(0, 2 * steps)
    def _(n):
        loaded = [
            (w[i], gv[i], xr[:, i].reshape(tokens, HD), qv[i], kv[i]) for i in group(n)
        ]
        results = [score_grads(*values) for values in loaded]
        for i, (for_queries, for_keys) in zip(group(n), results):
            qo[n // steps, :, columns(i % heads)] = for_queries
            ko[n // steps, :, columns(i % heads)] = for_keys

    @pl.when(section > 0)
    def _():
        for h in range(heads):
            relay0(h).wait_send()
            relay1(h).wait_send()

    for j in range(len(STEPS)):
        exchange(j).wait_send()

    @pl.when(jnp.logical_not(is_last))
    def _():
        for h in range(heads):
            relay1(h).wait_recv()

    @pl.when(is_last)
    def _():
        landed[...] = jnp.zeros_like(landed)


def place(heads, landed, qo, ko, next_hbm, qg_hbm, kg_hbm, next_sem, q_sem, k_sem):
    copies = []
    for m in range(2):
        copies.append(pltpu.make_async_copy(qo.at[m], qg_hbm.at[0, m], q_sem.at[m]))
        copies.append(pltpu.make_async_copy(ko.at[m], kg_hbm.at[0, m], k_sem.at[m]))
    for h in range(heads):
        copies.append(
            pltpu.make_async_copy(
                landed.at[h], next_hbm.at[0, :, pl.ds(h * HD, HD)], next_sem.at[h]
            )
        )
    for copy in copies:
        copy.start()
    for copy in copies:
        copy.wait()


def solution(mesh):
    sections = mesh.shape["section"]

    def local(*arguments):
        grad_in, loss_grad, queries, attn_keys, stored_input, block_scales = arguments
        tokens, width = loss_grad.shape
        heads = width // HD
        rows = stored_input.shape[2]
        both = 2 * heads
        parts = len(STEPS) + 1
        bf16, dma = jnp.bfloat16, pltpu.SemaphoreType.DMA
        anywhere = pl.BlockSpec(memory_space=pltpu.HBM)
        piece = (tokens, HD)
        inside = pl.BlockSpec(memory_space=pltpu.VMEM)
        held = pl.pallas_call(
            functools.partial(kernel, sections, heads),
            out_shape=(
                jax.ShapeDtypeStruct((heads, *piece), bf16),
                jax.ShapeDtypeStruct(queries.shape[1:], bf16),
                jax.ShapeDtypeStruct(attn_keys.shape[1:], bf16),
            ),
            in_specs=[anywhere] * 6,
            out_specs=(inside,) * 3,
            scratch_shapes=[
                pltpu.VMEM(stored_input.shape[1:], bf16),
                pltpu.VMEM(block_scales.shape[1:], bf16),
                pltpu.VMEM((both, *piece), bf16),
                pltpu.VMEM((both, *piece), bf16),
                pltpu.VMEM((both, *piece), bf16),
                pltpu.VMEM((parts, both, rows, HD), bf16),
                pltpu.VMEM((parts, both, rows, HD), bf16),
                pltpu.VMEM((both, tokens, tokens), jnp.float32),
                pltpu.VMEM((heads, *piece), bf16),
                pltpu.VMEM((heads, *piece), bf16),
                dma, dma, dma((both,)), dma((both,)), dma((both,)), dma,
                dma((len(STEPS),)), dma((len(STEPS),)),
                dma((heads,)), dma((heads,)), dma((heads,)),
            ],
            compiler_params=pltpu.CompilerParams(
                collective_id=0, has_side_effects=True, vmem_limit_bytes=24 * 2**20
            ),
            name="relay_attention",
        )(*(pltpu.with_memory_space_constraint(a, pltpu.HBM) for a in arguments))
        return pl.pallas_call(
            functools.partial(place, heads),
            out_shape=(
                jax.ShapeDtypeStruct(grad_in.shape, bf16),
                jax.ShapeDtypeStruct(queries.shape, bf16),
                jax.ShapeDtypeStruct(attn_keys.shape, bf16),
            ),
            in_specs=[inside] * 3,
            out_specs=(anywhere,) * 3,
            scratch_shapes=[dma((heads,)), dma((2,)), dma((2,))],
            compiler_params=pltpu.CompilerParams(vmem_limit_bytes=8 * 2**20),
            name="place",
        )(*held)

    return jax.shard_map(
        local,
        mesh=mesh,
        in_specs=(
            P("section", None, "tensor"),
            P(None, "tensor"),
            P("section", None, None, "tensor"),
            P("section", None, None, "tensor"),
            P("section", None, "tensor", None),
            P("section", None, "tensor", None),
        ),
        out_specs=(
            P("section", None, "tensor"),
            P("section", None, None, "tensor"),
            P("section", None, None, "tensor"),
        ),
        check_vma=False,
    )
```
